32 devices in a mesh: groups: 2 (over y), stream: 4 (over z), tensor: 2 (over x), sub: 2 (over core).
Axes of the slice: x: 2, y: 2, z: 4, core: 2. Of those that a mesh axis runs over, the one named last changes fastest.
Arguments:
- lm_query: bfloat16 [192, 3584], P(('groups', 'stream', 'sub'), 'tensor'), parts along dimension 0, may hold values from -6 to 6
- lm_cache: bfloat16 [192, 64, 2, 512], P(('groups', 'stream', 'sub'), None, None, 'tensor'), parts along dimension 0, may hold values from -6 to 6
- language_new_pair: bfloat16 [192, 2, 512], P(('groups', 'stream', 'sub'), None, 'tensor'), parts along dimension 0, may hold values from -6 to 6
- lm_lengths: int32 [192], P('groups'), parts along dimension 0, may hold values from 21 to 64, as said below
- lm_resid: bfloat16 [192, 3584], P(('groups', 'stream'), 'sub'), parts along dimension 0, may hold values from -18 to 18
- lm_wo: bfloat16 [3584, 3584], P('tensor', 'sub'), may hold values from -0.09375 to 0.09375
- lm_gain: bfloat16 [3584], P('sub'), may hold values from 0.5 to 1.5
- lm_adapt: bfloat16 [3584, 1024], P('sub', 'tensor'), may hold values from -0.09375 to 0.09375
- det_noise: bfloat16 [192, 30, 1024], P(('groups', 'stream'), None, ('tensor', 'sub')), parts along dimension 0, may hold values from -18 to 18
- det_pending: bfloat16 [192, 29, 1024], P(('groups', 'stream'), None, ('tensor', 'sub')), parts along dimension 0, may hold values from -6 to 6
- det_cache: bfloat16 [8, 24, 60, 2, 1024], P(('groups', 'stream'), None, None, None, ('tensor', 'sub')), parts along dimension 0, may hold values from -6 to 6
- det_qkv: bfloat16 [3, 1024, 1024], P(None, None, ('tensor', 'sub')), may hold values from -0.1875 to 0.1875
- det_out: bfloat16 [1024, 1024], P(('tensor', 'sub')), may hold values from -0.1875 to 0.1875
- det_gain: bfloat16 [1024], replicated, may hold values from 0.5 to 1.5
- complete: int32 [192], P('groups'), parts along dimension 0, may hold values from 0 to 1, as said below
- owner: int32 [192], P('groups'), parts along dimension 0, may hold values from 0 to 3, as said below
- prev_owner: int32 [192], P('groups'), parts along dimension 0, may hold values from 0 to 3, as said below
Outputs:
- lm_hidden: bfloat16 [192, 3584], P(('groups', 'stream'), 'sub'), parts along dimension 0
- new_state: bfloat16 [8, 4, 6, 30, 1024], P(('groups', 'stream'), None, None, None, ('tensor', 'sub')), parts along dimension 0
The draws below stay inside these ranges and needn't reach their ends.
There are 2 independent parts, one for each index of `groups`. The reference program is written for one: setup_inputs(seed, part) draws one part's arguments, and reference() takes and returns one part's arrays. A program takes and returns all parts, laid end to end along the dimension named above; an argument that names none is the same for every part. Nothing has to cross between parts.
Inputs may be any that keep to these rules, and one draw needn't show every extreme that they name: `lm_lengths`: some stream has exactly 64 valid positions. From one stream shard (streams j * 24 to (j + 1) * 24 - 1) at most 6 complete streams have the same owner, and some owner receives exactly 6 from every shard. `owner`: only the owners of complete streams matter. `prev_owner`: every owner holds exactly 24 streams' caches; at most 6 complete streams share one pair of previous and new owner, and for some new owner that many come from every previous owner.
All inputs are finite; a program needn't handle non-finite values.
Results may differ from the reference program's by a relative error of at most 0.006.
Values may be sent and summed in bfloat16 or wider, within the bound.
No kernel may reach another device: no remote copies, remote signals or barrier semaphores. Data moves between devices by JAX's collectives and lax.ppermute only.
A program may use at most 128 MiB of HBM per device.

```python
import jax
import jax.numpy as jnp
from jax import lax

D = 3584
QUERY_HEADS = 28
KEY_VALUE_HEADS = 4
HEAD_WIDTH = 128
C = 1024
DH = 16
DHD = 64
SPAN = 30
PAST = 2
CACHE_LENGTH = 64
SLOTS = 6
OWNERS = 4
SHARD_STREAMS = 24
STREAM_COUNT = 96


def routing_tables(base_key):
    base_key = jax.random.fold_in(base_key, 7321)
    k_count, k_full, k_perm, place_subkey, k_token, k_spare = jax.random.split(base_key, 6)
    counts = jax.random.randint(k_count, (OWNERS, OWNERS), 0, SLOTS + 1)
    full_owner = jax.random.randint(k_full, (), 0, OWNERS)
    counts = jnp.where(jnp.arange(OWNERS)[None, :] == full_owner, SLOTS, counts)
    chosen_index = jnp.arange(SLOTS)[None, None, :] < counts[:, :, None]
    perm_keys = jax.random.split(k_perm, OWNERS * SLOTS)
    prev_perm = jax.vmap(lambda subkey: jax.random.permutation(subkey, OWNERS))(perm_keys)
    prev_perm = prev_perm.reshape(OWNERS, SLOTS, OWNERS)
    prev_flat = jnp.transpose(prev_perm, (2, 0, 1)).reshape(OWNERS, SHARD_STREAMS)
    is_valid = chosen_index.reshape(OWNERS, SHARD_STREAMS)
    owner_flat = jnp.broadcast_to(jnp.arange(OWNERS)[None, :, None], (OWNERS, OWNERS, SLOTS)).reshape(OWNERS, SHARD_STREAMS)
    prev_match = jnp.logical_and(is_valid[..., None], prev_flat[..., None] == jnp.arange(OWNERS)[None, None, :])
    prev_load = jnp.sum(prev_match.astype(jnp.int32), axis=(0, 1))
    token_owner = jnp.repeat(jnp.arange(OWNERS), SHARD_STREAMS)
    token_rank = jnp.tile(jnp.arange(SHARD_STREAMS), OWNERS)
    is_used = token_rank < prev_load[token_owner]
    scores = jax.random.randint(k_token, (STREAM_COUNT,), 0, 2 ** 20)
    scores = jnp.where(is_used, 2 ** 21, scores)
    token_order = jnp.argsort(scores, stable=True)
    invalid = jnp.logical_not(is_valid).reshape(-1)
    spare_rank = jnp.cumsum(invalid.astype(jnp.int32)) - 1
    spare_prev = token_owner[token_order[jnp.clip(spare_rank, 0, STREAM_COUNT - 1)]]
    prev_all = jnp.where(invalid, spare_prev, prev_flat.reshape(-1))
    spare_owner = jax.random.randint(k_spare, (STREAM_COUNT,), 0, OWNERS)
    owner_all = jnp.where(invalid, spare_owner, owner_flat.reshape(-1))
    place_keys = jax.random.split(place_subkey, OWNERS)
    places = jax.vmap(lambda subkey: jax.random.permutation(subkey, SHARD_STREAMS))(place_keys)
    target = (jnp.arange(OWNERS)[:, None] * SHARD_STREAMS + places).reshape(-1)
    done_flags = jnp.zeros((STREAM_COUNT,), jnp.int32).at[target].set(is_valid.reshape(-1).astype(jnp.int32))
    owners = jnp.zeros((STREAM_COUNT,), jnp.int32).at[target].set(owner_all.astype(jnp.int32))
    prev_ids = jnp.zeros((STREAM_COUNT,), jnp.int32).at[target].set(prev_all.astype(jnp.int32))
    return (done_flags, owners, prev_ids)


def draw_complete(key, part):
    return routing_tables(key)[0]


def draw_owner(key, part):
    return routing_tables(key)[1]


def draw_prev_owner(key, part):
    return routing_tables(key)[2]


def draw_lm_lengths(key, part):
    length_key = jax.random.fold_in(key, 911)
    k_lengths, k_longest = jax.random.split(length_key, 2)
    lengths = jax.random.randint(k_lengths, (STREAM_COUNT,), CACHE_LENGTH // 3, CACHE_LENGTH + 1)
    longest = jax.random.randint(k_longest, (), 0, STREAM_COUNT)
    return jnp.where(jnp.arange(STREAM_COUNT) == longest, CACHE_LENGTH, lengths).astype(jnp.int32)


def standard_normal(key, shape):
    return jnp.clip(jax.random.normal(key, shape, jnp.float32), -6.0, 6.0)


def column_scale(width):
    position = jnp.arange(width).astype(jnp.float32) / max(width - 1, 1)
    return 0.5 + 2.0 * position


def draw_lm_resid(key, part):
    value_rows = standard_normal(jax.random.fold_in(key, 107), (STREAM_COUNT, D))
    value_rows = value_rows * column_scale(D)[None, :]
    return value_rows.astype(jnp.bfloat16)


def draw_lm_query(key, part):
    value_rows = standard_normal(jax.random.fold_in(key, 101), (STREAM_COUNT, QUERY_HEADS * HEAD_WIDTH))
    return value_rows.astype(jnp.bfloat16)


def draw_lm_cache(key, part):
    value_rows = standard_normal(jax.random.fold_in(key, 102), (STREAM_COUNT, CACHE_LENGTH, 2, KEY_VALUE_HEADS * HEAD_WIDTH))
    return value_rows.astype(jnp.bfloat16)


def draw_det_noise(key, part):
    value_rows = standard_normal(jax.random.fold_in(key, 103), (STREAM_COUNT, SPAN, C))
    value_rows = value_rows * column_scale(C)[None, None, :]
    return value_rows.astype(jnp.bfloat16)


def draw_det_cache(key, part):
    value_rows = standard_normal(jax.random.fold_in(key, 104), (OWNERS, SHARD_STREAMS, PAST * SPAN, 2, C))
    return value_rows.astype(jnp.bfloat16)


def draw_det_qkv(key, part):
    value_rows = standard_normal(jax.random.fold_in(key, 105), (3, C, C)) * C ** (-0.5)
    return value_rows.astype(jnp.bfloat16)


def block_levels(own_key, extent, cuts, low, high):
    level, own = 1.0, jax.random.fold_in(own_key, 6)
    for dim, parts in cuts:
        heights = jnp.exp(jax.random.uniform(jax.random.fold_in(own, dim), (parts,), jnp.float32, low / len(cuts), high / len(cuts)))
        level = level * jnp.repeat(heights, extent[dim] // parts).reshape([-1 if axis == dim else 1 for axis in range(len(extent))])
    return level


def centred(stream_key, dims, scale, reach, cuts=(), kind=jnp.bfloat16):
    entries = jax.random.normal(stream_key, dims, jnp.float32) * scale
    if len(cuts) > 0:
        entries = block_levels(stream_key, dims, cuts, -0.22, 0.18) * entries
    return jnp.clip(entries, min=-reach, max=reach).astype(kind)


def setup_inputs(seed: int = 0, part: int = 0) -> dict:
    key_of = jax.random.split(jax.random.key(seed), 18)
    own_keys = jax.random.split(jax.random.fold_in(key_of[17], part), 18)
    lm_query = draw_lm_query(jax.random.fold_in(jax.random.fold_in(key_of[17], part), 71), part)
    lm_cache = draw_lm_cache(jax.random.fold_in(jax.random.fold_in(key_of[17], part), 71), part)
    language_new_pair = centred(own_keys[2], (STREAM_COUNT, 2, KEY_VALUE_HEADS * HEAD_WIDTH), 1.0, 6.0, ((0, 8), (2, 2)))
    lm_lengths = draw_lm_lengths(jax.random.fold_in(jax.random.fold_in(key_of[17], part), 71), part)
    lm_resid = draw_lm_resid(jax.random.fold_in(jax.random.fold_in(key_of[17], part), 71), part)
    lm_wo = centred(key_of[5], (QUERY_HEADS * HEAD_WIDTH, D), (QUERY_HEADS * HEAD_WIDTH) ** -0.5, 0.09375, ((0, 2), (1, 2)))
    lm_gain = jnp.clip(1.0 + 0.1 * jax.random.normal(key_of[6], (D,), jnp.float32), 0.5, 1.5).astype(jnp.bfloat16)
    lm_adapt = centred(key_of[7], (D, C), D ** -0.5, 0.09375, ((0, 2), (1, 2)))
    det_noise = draw_det_noise(jax.random.fold_in(jax.random.fold_in(key_of[17], part), 71), part)
    det_pending = centred(own_keys[9], (STREAM_COUNT, SPAN - 1, C), 1.0, 6.0, ((0, 4), (2, 4)))
    det_cache = draw_det_cache(jax.random.fold_in(jax.random.fold_in(key_of[17], part), 71), part)
    det_qkv = draw_det_qkv(jax.random.fold_in(key_of[17], 71), part)
    det_out = centred(key_of[12], (C, C), C ** -0.5, 0.1875, ((0, 4),))
    det_gain = jnp.clip(1.0 + 0.1 * jax.random.normal(key_of[13], (C,), jnp.float32), 0.5, 1.5).astype(jnp.bfloat16)
    complete = draw_complete(jax.random.fold_in(jax.random.fold_in(key_of[17], part), 71), part)
    owner = draw_owner(jax.random.fold_in(jax.random.fold_in(key_of[17], part), 71), part)
    prev_owner = draw_prev_owner(jax.random.fold_in(jax.random.fold_in(key_of[17], part), 71), part)
    return dict(lm_query=lm_query, lm_cache=lm_cache, language_new_pair=language_new_pair, lm_lengths=lm_lengths, lm_resid=lm_resid, lm_wo=lm_wo, lm_gain=lm_gain, lm_adapt=lm_adapt, det_noise=det_noise, det_pending=det_pending, det_cache=det_cache, det_qkv=det_qkv, det_out=det_out, det_gain=det_gain, complete=complete, owner=owner, prev_owner=prev_owner)


step_size = 0.5
epsilon = 1e-06

def rounded(value_rows):
    return lax.optimization_barrier(value_rows.astype(jnp.bfloat16)).astype(jnp.float32)

def decode_attention(query, cache, fresh, lengths):
    streams = query.shape[0]
    kv_heads = cache.shape[-1] // HEAD_WIDTH
    mixing_ratio = QUERY_HEADS // KEY_VALUE_HEADS
    queries = query.astype(jnp.float32).reshape(streams, kv_heads, mixing_ratio, HEAD_WIDTH)
    past_keys = cache[:, :, 0, :].astype(jnp.float32).reshape(streams, CACHE_LENGTH, kv_heads, HEAD_WIDTH)
    past_values = cache[:, :, 1, :].astype(jnp.float32).reshape(streams, CACHE_LENGTH, kv_heads, HEAD_WIDTH)
    fresh_key_rows = fresh[:, 0, :].astype(jnp.float32).reshape(streams, kv_heads, HEAD_WIDTH)
    new_values = fresh[:, 1, :].astype(jnp.float32).reshape(streams, kv_heads, HEAD_WIDTH)
    scale = HEAD_WIDTH ** (-0.5)
    past_scores = jnp.einsum('skgd,slkd->skgl', queries, past_keys) * scale
    new_scores = jnp.einsum('skgd,skd->skg', queries, fresh_key_rows) * scale
    visible = (jnp.arange(CACHE_LENGTH)[None, :] < lengths[:, None])[:, None, None, :]
    masked = jnp.where(visible, past_scores, -1e+30)
    top = jnp.maximum(lax.optimization_barrier(jnp.max(masked, axis=-1)), new_scores)
    past_weights = jnp.where(visible, jnp.exp(masked - top[..., None]), 0.0)
    new_weights = jnp.exp(new_scores - top)
    total = lax.optimization_barrier(jnp.sum(past_weights, axis=-1)) + new_weights
    mixed = jnp.einsum('skgl,slkd->skgd', rounded(past_weights), past_values)
    mixed = mixed + rounded(new_weights)[..., None] * new_values[:, :, None, :]
    return (mixed / total[..., None]).reshape(streams, kv_heads * mixing_ratio * HEAD_WIDTH).astype(jnp.bfloat16)

def flow_step(noise, span, cache, live, det_qkv, det_out, det_gain):
    slots = noise.shape[0]
    past_len = cache.shape[1]
    state = noise.astype(jnp.float32) + span.astype(jnp.float32)
    mean_square = lax.optimization_barrier(jnp.mean(state * state, axis=-1, keepdims=True))
    normed = (state * lax.rsqrt(mean_square + epsilon) * det_gain.astype(jnp.float32)).astype(jnp.bfloat16)
    projected = jnp.einsum('ntc,kce->ntke', normed.astype(jnp.float32), det_qkv.astype(jnp.float32)).astype(jnp.bfloat16)
    queries = projected[:, :, 0].astype(jnp.float32).reshape(slots, SPAN, DH, DHD)
    keys = jnp.concatenate([cache[:, :, 0], projected[:, :, 1]], axis=1).astype(jnp.float32)
    value_rows = jnp.concatenate([cache[:, :, 1], projected[:, :, 2]], axis=1).astype(jnp.float32)
    keys = keys.reshape(slots, past_len + SPAN, DH, DHD)
    value_rows = value_rows.reshape(slots, past_len + SPAN, DH, DHD)
    scores = jnp.einsum('nthd,nlhd->nhtl', queries, keys) * DHD ** (-0.5)
    top = lax.optimization_barrier(jnp.max(scores, axis=-1, keepdims=True))
    weights = jnp.exp(scores - top)
    total = lax.optimization_barrier(jnp.sum(weights, axis=-1))
    mixed = jnp.einsum('nhtl,nlhd->nthd', rounded(weights), value_rows)
    mixed = (mixed / jnp.transpose(total, (0, 2, 1))[..., None]).reshape(slots, SPAN, C).astype(jnp.bfloat16)
    mixing = jnp.einsum('ntc,ce->nte', mixed.astype(jnp.float32), det_out.astype(jnp.float32))
    velocity = span.astype(jnp.float32) - noise.astype(jnp.float32) + mixing
    updated = (noise.astype(jnp.float32) + step_size * velocity) * live[:, None, None]
    return updated.astype(jnp.bfloat16)

def exclusive_rank(hot, reduce_axis):
    return lax.optimization_barrier(jnp.sum((jnp.cumsum(hot, axis=reduce_axis) - hot) * hot, axis=-1))

def reference(lm_query, lm_cache, language_new_pair, lm_lengths, lm_resid, lm_wo, lm_gain, lm_adapt, det_noise, det_pending, det_cache, det_qkv, det_out, det_gain, complete, owner, prev_owner):
    attention = decode_attention(lm_query, lm_cache, language_new_pair, lm_lengths)
    mixing = jnp.dot(attention, lm_wo, preferred_element_type=jnp.float32)
    hidden = (lm_resid.astype(jnp.float32) + mixing).astype(jnp.bfloat16)
    hidden_wide = hidden.astype(jnp.float32)
    mean_square = lax.optimization_barrier(jnp.mean(hidden_wide * hidden_wide, axis=-1, keepdims=True))
    normed = (hidden_wide * lax.rsqrt(mean_square + epsilon) * lm_gain.astype(jnp.float32)).astype(jnp.bfloat16)
    cond_new = jnp.dot(normed, lm_adapt, preferred_element_type=jnp.float32).astype(jnp.bfloat16)
    span = jnp.concatenate([det_pending, cond_new[:, None, :]], axis=1)
    done = complete == 1
    owner_range = jnp.arange(OWNERS).astype(jnp.int32)
    owner_hot = jnp.logical_and(owner[:, None] == owner_range[None, :], done[:, None]).astype(jnp.int32)
    by_home = owner_hot.reshape(OWNERS, SHARD_STREAMS, OWNERS)
    home_rank = lax.optimization_barrier(jnp.sum((jnp.cumsum(by_home, axis=1) - by_home).reshape(STREAM_COUNT, OWNERS) * owner_hot, axis=-1))
    prev_hot = (prev_owner[:, None] == owner_range[None, :]).astype(jnp.int32)
    cache_slot = exclusive_rank(prev_hot, 0)
    stream_ids = jnp.arange(STREAM_COUNT).astype(jnp.int32)
    total_slots = OWNERS * OWNERS * SLOTS
    slot_index = (owner * OWNERS + stream_ids // SHARD_STREAMS) * SLOTS + home_rank
    slot_index = jnp.where(done, slot_index, total_slots).astype(jnp.int32)
    stream_of_slot = jnp.full((total_slots,), -1, jnp.int32).at[slot_index].set(stream_ids, mode='drop')
    present = (stream_of_slot >= 0).astype(jnp.float32)
    source = jnp.maximum(stream_of_slot, 0)

    def one_owner(owner_slots):
        sources, live = owner_slots
        return flow_step(det_noise[sources], span[sources], det_cache[prev_owner[sources], cache_slot[sources]], live, det_qkv, det_out, det_gain)
    new_state = lax.map(one_owner, (source.reshape(OWNERS, OWNERS * SLOTS), present.reshape(OWNERS, OWNERS * SLOTS)))
    return (hidden, new_state.reshape(OWNERS, OWNERS, SLOTS, SPAN, C))
```

```python
import functools

import jax
import jax.numpy as jnp
from jax import lax
from jax.experimental import pallas as pl
from jax.experimental.pallas import tpu as pltpu
from jax.sharding import PartitionSpec as P

D = 3584
QUERY_HEADS = 28
KEY_VALUE_HEADS = 4
HEAD_WIDTH = 128
C = 1024
DHD = 64
SLOTS = 6

LANES = 128
step_size = 0.5
epsilon = 1e-06

VMEM = pl.BlockSpec(memory_space=pltpu.VMEM)
SMEM = pl.BlockSpec(memory_space=pltpu.SMEM)
ANY = pl.BlockSpec(memory_space=pl.ANY)
PARAMS = pltpu.CompilerParams(vmem_limit_bytes=48 << 20)


def rounded(value_rows):
    return lax.optimization_barrier(value_rows.astype(jnp.bfloat16)).astype(jnp.float32)


def decode_attention(query, cache, fresh, visible):
    streams = query.shape[0]
    positions = cache.shape[1]
    kv_heads = cache.shape[-1] // HEAD_WIDTH
    mixing_ratio = QUERY_HEADS // KEY_VALUE_HEADS
    queries = query.reshape(streams, kv_heads, mixing_ratio, HEAD_WIDTH)
    past_keys = cache[:, :, 0, :].reshape(streams, positions, kv_heads, HEAD_WIDTH)
    past_values = cache[:, :, 1, :].reshape(streams, positions, kv_heads, HEAD_WIDTH)
    fresh_key_rows = fresh[:, 0, :].reshape(streams, kv_heads, HEAD_WIDTH)
    new_values = fresh[:, 1, :].reshape(streams, kv_heads, HEAD_WIDTH)
    scale = HEAD_WIDTH ** (-0.5)
    past_scores = (
        jnp.einsum("skgd,slkd->skgl", queries, past_keys, preferred_element_type=jnp.float32)
        * scale
    )
    new_scores = (
        jnp.einsum("skgd,skd->skg", queries, fresh_key_rows, preferred_element_type=jnp.float32)
        * scale
    )
    window = visible[:, None, None, :]
    masked = jnp.where(window, past_scores, -1e30)
    top = jnp.maximum(jnp.max(masked, axis=-1), new_scores)
    past_weights = jnp.where(window, jnp.exp(masked - top[..., None]), 0.0)
    new_weights = jnp.exp(new_scores - top)
    total = jnp.sum(past_weights, axis=-1) + new_weights
    mixed = jnp.einsum(
        "skgl,slkd->skgd",
        past_weights.astype(jnp.bfloat16),
        past_values,
        preferred_element_type=jnp.float32,
    )
    mixed = mixed + rounded(new_weights)[..., None] * new_values.astype(jnp.float32)[:, :, None, :]
    return (
        (mixed / total[..., None])
        .reshape(streams, kv_heads * mixing_ratio * HEAD_WIDTH)
        .astype(jnp.bfloat16)
    )


def exclusive_rank(hot, reduce_axis):
    return jnp.sum((jnp.cumsum(hot, axis=reduce_axis) - hot) * hot, axis=-1)


def exchange(value, axis, distance):
    return lax.ppermute(value, axis, [(i, i ^ distance) for i in range(lax.axis_size(axis))])


def shift(value, axis, distance):
    size = lax.axis_size(axis)
    return lax.ppermute(value, axis, [(i, (i + distance) % size) for i in range(size)])


def tree_sum(values):
    while len(values) > 1:
        values = [values[i] + values[i + 1] for i in range(0, len(values), 2)]
    return values[0]


def dispatch_kernel(owners, span, tokens, streams, table, noise, pending, cache, *rest):
    states = rest[:owners]
    caches = rest[owners : 2 * owners]
    wide, sems = rest[2 * owners :]
    width = noise.shape[1]

    def copy(slot):
        target = caches[slot // SLOTS].at[slot % SLOTS]
        return pltpu.make_async_copy(cache.at[table[1, slot]], target, sems.at[slot])

    for slot in range(owners * SLOTS):
        copy(slot).start()
    early = (span - 1) * streams
    for part in range(width // LANES):
        lanes = slice(part * LANES, (part + 1) * LANES)
        wide[part, :early] = noise[:early, lanes].astype(jnp.float32) + pending[
            :, lanes
        ].astype(jnp.float32)
        wide[part, early : span * streams] = noise[early:, lanes].astype(jnp.float32)
        wide[part, span * streams :] = jnp.zeros(
            ((tokens - span) * streams, LANES), jnp.float32
        )
        for slot in range(owners * SLOTS):
            rows = wide[part, pl.ds(table[0, slot], tokens, stride=streams), :]
            first = slot % SLOTS * tokens
            states[slot // SLOTS][first : first + tokens, lanes] = rows.astype(jnp.bfloat16)
    for slot in range(owners * SLOTS):
        copy(slot).wait()


def project_kernel(block_rows, piece_count, index, *refs):
    pieces = refs[:piece_count]
    gain, weights, q_out, k_out, v_out = refs[piece_count:]
    width = pieces[0].shape[1]

    def block(step, carry):
        rows = pl.ds(pl.multiple_of(step * block_rows, block_rows), block_rows)
        values = [piece[rows, :].astype(jnp.float32) for piece in pieces]
        squares = functools.reduce(
            jnp.add, [jnp.sum(value * value, axis=1, keepdims=True) for value in values]
        )
        scale = lax.rsqrt(squares / C + epsilon)
        sums = [jnp.zeros((block_rows, width), jnp.float32) for _ in range(3)]
        for at, value in enumerate(values):
            part = index[at]
            normed = (value * scale * gain[part]).astype(jnp.bfloat16)
            features = pl.ds(pl.multiple_of(part * width, width), width)
            for which in range(3):
                sums[which] += jnp.dot(
                    normed, weights[which, features, :], preferred_element_type=jnp.float32
                )
        for out, value in zip((q_out, k_out, v_out), sums):
            out[rows, :] = value.astype(jnp.bfloat16)
        return carry

    lax.fori_loop(0, pieces[0].shape[0] // block_rows, block, 0)


def late_kernel(owners, parts, index, picker, gathered, gain, weights, q_out, k_out, v_out, s_out):
    width = gathered.shape[2]

    def select(part):
        rows = jnp.concatenate(
            [gathered[home * parts + part].astype(jnp.float32) for home in range(owners)], axis=0
        )
        return jnp.dot(
            picker[...], rows.astype(jnp.bfloat16), preferred_element_type=jnp.float32
        )

    values = [select(part) for part in range(parts)]
    squares = functools.reduce(
        jnp.add, [jnp.sum(value * value, axis=1, keepdims=True) for value in values]
    )
    scale = lax.rsqrt(squares / C + epsilon)
    sums = [jnp.zeros((picker.shape[0], width), jnp.float32) for _ in range(3)]
    for part, value in enumerate(values):
        normed = (value * scale * gain[part]).astype(jnp.bfloat16)
        for which in range(3):
            sums[which] += jnp.dot(
                normed,
                weights[which, part * width : (part + 1) * width, :],
                preferred_element_type=jnp.float32,
            )
    for out, value in zip((q_out, k_out, v_out), sums):
        out[...] = value.astype(jnp.bfloat16).astype(jnp.float32)
    s_out[...] = select(index[0])


def attend_kernel(
    owners, span, tokens, first_slot, count, unroll, tensor_count, sub_count,
    index, table, q_rows, k_rows, v_rows, q_late, k_late, v_late, out_weights, *rest,
):
    caches = rest[:owners]
    keep_out, send_out, staged, keys, values, mixed, sems = rest[owners:]
    past = caches[0].shape[1]
    width = q_rows.shape[1]
    heads = width // DHD
    key_rows = keys.shape[1]
    own = key_rows - tokens

    def start(at, carry):
        place = table[2, first_slot + at]
        for which in range(owners):
            @pl.when(place // SLOTS == which)
            def _():
                pltpu.make_async_copy(
                    caches[which].at[place - which * SLOTS], staged.at[at], sems.at[at]
                ).start()
        return carry

    lax.fori_loop(0, count, start, 0, unroll=unroll)
    if own > past:
        filler = jnp.zeros((unroll, own - past, width), jnp.bfloat16)
        keys[:, past:own, :] = filler
        values[:, past:own, :] = filler
    lane_head = lax.broadcasted_iota(jnp.int32, (tokens, width), 1) // DHD
    late = lax.broadcasted_iota(jnp.int32, (tokens, width), 0) == span - 1
    key_at = lax.broadcasted_iota(jnp.int32, (heads * tokens, key_rows), 1)
    valid = jnp.logical_or(
        key_at < past, jnp.logical_and(key_at >= own, key_at < own + span)
    )

    def with_late(rows_ref, late_ref, slot):
        rows = rows_ref[pl.ds(pl.multiple_of(slot * tokens, tokens), tokens), :]
        return jnp.where(late, late_ref[pl.ds(slot, 1), :], rows.astype(jnp.float32))

    def attend(at, buffer):
        slot = first_slot + at
        pltpu.make_async_copy(caches[0].at[0], staged.at[at], sems.at[at]).wait()
        pairs = staged[at].reshape(past, 2 * width)
        keys[buffer, :past, :] = pairs[:, :width]
        values[buffer, :past, :] = pairs[:, width:]
        keys[buffer, own:, :] = with_late(k_rows, k_late, slot).astype(jnp.bfloat16)
        values[buffer, own:, :] = with_late(v_rows, v_late, slot).astype(jnp.bfloat16)
        queries = with_late(q_rows, q_late, slot)
        stacked = jnp.concatenate(
            [jnp.where(lane_head == head, queries, 0.0) for head in range(heads)], axis=0
        ).astype(jnp.bfloat16)
        scores = lax.dot_general(
            stacked, keys[buffer], (((1,), (1,)), ((), ())), preferred_element_type=jnp.float32
        ) * DHD ** (-0.5)
        scores = jnp.where(valid, scores, -1e30)
        top = jnp.max(scores, axis=1, keepdims=True)
        weights = jnp.exp(scores - top)
        total = jnp.sum(weights, axis=1, keepdims=True)
        sums = jnp.dot(
            weights.astype(jnp.bfloat16), values[buffer], preferred_element_type=jnp.float32
        )
        sums = sums / total
        result = sums[:tokens]
        for head in range(1, heads):
            result = jnp.where(
                lane_head == head, sums[head * tokens : (head + 1) * tokens], result
            )
        mixed[pl.ds(pl.multiple_of(at * tokens, tokens), tokens), :] = result.astype(jnp.bfloat16)

    def group(step, carry):
        for buffer in range(unroll):
            attend(step * unroll + buffer, buffer)
        return carry

    lax.fori_loop(0, count // unroll, group, 0, unroll=count // unroll <= 2)
    my_tensor, my_sub = index[0] // sub_count, index[0] % sub_count
    for step in range(tensor_count):
        for out, sub in ((keep_out, my_sub), (send_out, 1 - my_sub)):
            part = jnp.bitwise_xor(my_tensor, step) * sub_count + sub
            lanes = pl.ds(pl.multiple_of(part * width, width), width)
            product = jnp.dot(
                mixed[...], out_weights[:, lanes], preferred_element_type=jnp.float32
            )
            out[step] = product.astype(jnp.bfloat16)


def shards(
    lm_query,
    lm_cache,
    language_new_pair,
    lm_lengths,
    lm_resid,
    lm_wo,
    lm_gain,
    lm_adapt,
    det_noise,
    det_pending,
    det_cache,
    det_qkv,
    det_out,
    det_gain,
    complete,
    owner,
    prev_owner,
):
    owners = lax.axis_size("stream")
    tensor_count = lax.axis_size("tensor")
    sub_count = lax.axis_size("sub")
    parts = tensor_count * sub_count
    home = lax.axis_index("stream")
    my_tensor = lax.axis_index("tensor")
    my_sub = lax.axis_index("sub")
    part_index = my_tensor * sub_count + my_sub
    local_streams = lm_query.shape[0]
    shard_streams, span_len, col_width = det_noise.shape
    past_len = det_cache.shape[2]
    tokens = -(-span_len // 16) * 16
    slot_count = owners * SLOTS
    stream_total = owner.shape[0]

    stream_ids = jnp.arange(stream_total)
    owner_range = jnp.arange(owners)
    done = complete == 1
    owner_hot = jnp.logical_and(owner[:, None] == owner_range[None, :], done[:, None]).astype(
        jnp.int32
    )
    by_home = owner_hot.reshape(owners, shard_streams, owners)
    home_rank = jnp.sum(
        (jnp.cumsum(by_home, axis=1) - by_home).reshape(stream_total, owners) * owner_hot, axis=-1
    )
    prev_hot = (prev_owner[:, None] == owner_range[None, :]).astype(jnp.int32)
    cache_slot = exclusive_rank(prev_hot, 0)
    pair_key = prev_owner * owners + owner
    pair_hot = jnp.logical_and(
        pair_key[:, None] == jnp.arange(owners * owners)[None, :], done[:, None]
    ).astype(jnp.int32)
    pair_rank = exclusive_rank(pair_hot, 0)
    slot_range = jnp.arange(slot_count)
    stream_home = stream_ids // shard_streams
    away = jnp.where(owner >= home, owner - home, owner - home + owners)
    here = jnp.logical_and(done, stream_home == home)
    send_key = jnp.where(here, away * SLOTS + home_rank, -1)
    send_stream = jnp.sum(
        jnp.where(
            slot_range[:, None] == send_key[None, :], (stream_ids % shard_streams)[None, :], 0
        ),
        axis=1,
    )
    moving = jnp.logical_and(done, prev_owner == home)
    cache_key = jnp.where(moving, away * SLOTS + pair_rank, -1)
    send_cache = jnp.sum(
        jnp.where(slot_range[:, None] == cache_key[None, :], cache_slot[None, :], 0), axis=1
    )
    owned = jnp.logical_and(done, owner == home)
    from_home = jnp.where(home >= stream_home, home - stream_home, home - stream_home + owners)
    slot_key = jnp.where(owned, from_home * SLOTS + home_rank, -1)
    from_prev = jnp.where(home >= prev_owner, home - prev_owner, home - prev_owner + owners)
    slot_hot = slot_range[:, None] == slot_key[None, :]
    cache_place = jnp.sum(
        jnp.where(slot_hot, (from_prev * SLOTS + pair_rank)[None, :], 0), axis=1
    )
    live = jnp.sum(slot_hot.astype(jnp.float32), axis=1)
    picker = slot_hot.astype(jnp.bfloat16)
    table = jnp.stack([send_stream, send_cache, cache_place]).astype(jnp.int32)

    noise_rows = jnp.transpose(det_noise, (1, 0, 2)).reshape(span_len * shard_streams, col_width)
    pending_rows = jnp.transpose(det_pending, (1, 0, 2)).reshape(-1, col_width)
    shapes = [jax.ShapeDtypeStruct((SLOTS * tokens, col_width), jnp.bfloat16)] * owners
    shapes += [
        jax.ShapeDtypeStruct((SLOTS, past_len, 2, col_width), jnp.bfloat16)
    ] * owners
    packed = pl.pallas_call(
        functools.partial(dispatch_kernel, owners, span_len, tokens, shard_streams),
        out_shape=shapes,
        in_specs=[SMEM, VMEM, VMEM, ANY],
        out_specs=[VMEM] * (2 * owners),
        scratch_shapes=[
            pltpu.VMEM((col_width // LANES, tokens * shard_streams, LANES), jnp.float32),
            pltpu.SemaphoreType.DMA((slot_count,)),
        ],
        compiler_params=PARAMS,
        name="dispatch",
    )(table, noise_rows, pending_rows, det_cache.reshape(shard_streams, past_len, 2, col_width))
    arrived = [packed[0]] + [
        shift(packed[step], "stream", step) for step in range(1, owners)
    ]
    caches = [packed[owners]] + [
        shift(packed[owners + step], "stream", step) for step in range(1, owners)
    ]
    state = jnp.concatenate(arrived, axis=0)
    by_tensor = [state] + [exchange(state, "tensor", step) for step in range(1, tensor_count)]
    pieces = []
    piece_index = []
    for step in range(tensor_count):
        for flip in range(sub_count):
            pieces.append(by_tensor[step] if flip == 0 else exchange(by_tensor[step], "sub", flip))
            piece_index.append(
                jnp.bitwise_xor(my_tensor, step) * sub_count + jnp.bitwise_xor(my_sub, flip)
            )
    piece_index = jnp.stack(piece_index).astype(jnp.int32)
    gain_rows = det_gain.astype(jnp.float32).reshape(parts, 1, col_width)
    row_count = slot_count * tokens
    rows_shape = jax.ShapeDtypeStruct((row_count, col_width), jnp.bfloat16)
    q_rows, k_rows, v_rows = pl.pallas_call(
        functools.partial(project_kernel, SLOTS * tokens, parts),
        out_shape=[rows_shape] * 3,
        in_specs=[SMEM] + [VMEM] * (parts + 2),
        out_specs=[VMEM] * 3,
        compiler_params=PARAMS,
        name="project",
    )(piece_index, *pieces, gain_rows, det_qkv)

    first = (home * sub_count + my_sub) * local_streams
    lengths = lax.dynamic_slice_in_dim(lm_lengths, first, local_streams, 0)
    visible = jnp.arange(lm_cache.shape[1])[None, :] < lengths[:, None]
    attention = decode_attention(lm_query, lm_cache, language_new_pair, visible)
    other = exchange(attention, "sub", 1)
    attention_all = jnp.where(
        my_sub == 0,
        jnp.concatenate([attention, other], axis=0),
        jnp.concatenate([other, attention], axis=0),
    )
    partial_out = jnp.dot(attention_all, lm_wo, preferred_element_type=jnp.float32).astype(
        jnp.bfloat16
    )
    terms = [partial_out] + [
        exchange(partial_out, "tensor", step) for step in range(1, tensor_count)
    ]
    product = tree_sum([term.astype(jnp.float32) for term in terms])
    hidden = (lm_resid.astype(jnp.float32) + product).astype(jnp.bfloat16)
    hidden_wide = hidden.astype(jnp.float32)
    square_part = jnp.sum(hidden_wide * hidden_wide, axis=1)
    scaled = (hidden_wide * lm_gain.astype(jnp.float32)[None, :]).astype(jnp.bfloat16)
    cond_part = jnp.dot(scaled, lm_adapt, preferred_element_type=jnp.float32)
    bundle = jnp.concatenate(
        [cond_part, jnp.broadcast_to(square_part[:, None], (shard_streams, LANES))], axis=1
    )
    bundle = bundle + exchange(bundle, "sub", 1)
    tensor_width = lm_adapt.shape[1]
    inverse = lax.rsqrt(bundle[:, tensor_width : tensor_width + 1] / D + epsilon)
    cond_mine = lax.dynamic_slice_in_dim(bundle, my_sub * col_width, col_width, 1)
    cond_new = (cond_mine * inverse).astype(jnp.bfloat16)

    last_state = (
        det_noise[:, span_len - 1].astype(jnp.float32) + cond_new.astype(jnp.float32)
    ).astype(jnp.bfloat16)
    gathered = lax.all_gather(last_state, ("stream", "tensor", "sub"), axis=0)
    late_shape = jax.ShapeDtypeStruct((slot_count, col_width), jnp.float32)
    my_index = part_index.astype(jnp.int32).reshape(1)
    q_late, k_late, v_late, s_late = pl.pallas_call(
        functools.partial(late_kernel, owners, parts),
        out_shape=[late_shape] * 4,
        in_specs=[SMEM] + [VMEM] * 4,
        out_specs=[VMEM] * 4,
        compiler_params=PARAMS,
        name="late",
    )(my_index, picker, gathered, gain_rows, det_qkv)

    chunk_count = 4
    chunk_slots = slot_count // chunk_count
    unroll = SLOTS
    chunk_rows = chunk_slots * tokens
    key_rows = -(-past_len // 16) * 16 + tokens
    sums = []
    for chunk in range(chunk_count):
        piece_shape = jax.ShapeDtypeStruct((tensor_count, chunk_rows, col_width), jnp.bfloat16)
        keep, send = pl.pallas_call(
            functools.partial(
                attend_kernel, owners, span_len, tokens, chunk * chunk_slots, chunk_slots,
                unroll, tensor_count, sub_count,
            ),
            out_shape=[piece_shape] * 2,
            in_specs=[SMEM] * 2 + [VMEM] * 7 + [ANY] * owners,
            out_specs=[VMEM] * 2,
            scratch_shapes=[
                pltpu.VMEM((chunk_slots, past_len, 2, col_width), jnp.bfloat16),
                pltpu.VMEM((unroll, key_rows, col_width), jnp.bfloat16),
                pltpu.VMEM((unroll, key_rows, col_width), jnp.bfloat16),
                pltpu.VMEM((chunk_rows, col_width), jnp.bfloat16),
                pltpu.SemaphoreType.DMA((chunk_slots,)),
            ],
            compiler_params=PARAMS,
            name="attend",
        )(
            my_index, table, q_rows, k_rows, v_rows, q_late, k_late, v_late, det_out, *caches
        )
        both = keep.astype(jnp.float32) + exchange(send, "sub", 1).astype(jnp.float32)
        terms = [both[0]] + [
            exchange(both[step].astype(jnp.bfloat16), "tensor", step).astype(jnp.float32)
            for step in range(1, tensor_count)
        ]
        sums.append(tree_sum(terms))

    det_mixing = jnp.concatenate(sums, axis=0).reshape(slot_count, tokens, col_width)
    state_wide = state.astype(jnp.float32).reshape(slot_count, tokens, col_width)
    is_last = (jnp.arange(tokens) == span_len - 1)[None, :, None]
    state_wide = jnp.where(is_last, s_late[:, None, :], state_wide)
    updated = step_size * (state_wide + det_mixing) * live[:, None, None]
    updated = updated.astype(jnp.bfloat16)[:, :span_len].reshape(
        owners, SLOTS, span_len, col_width
    )
    order = home - jnp.arange(owners)
    order = jnp.where(order < 0, order + owners, order)
    updated = jnp.concatenate(
        [lax.dynamic_slice_in_dim(updated, order[j], 1, 0) for j in range(owners)], axis=0
    )
    return (hidden, updated[None])


def solution(mesh):
    return jax.shard_map(
        shards,
        mesh=mesh,
        in_specs=(
            P(("groups", "stream", "sub"), "tensor"),
            P(("groups", "stream", "sub"), None, None, "tensor"),
            P(("groups", "stream", "sub"), None, "tensor"),
            P("groups"),
            P(("groups", "stream"), "sub"),
            P("tensor", "sub"),
            P("sub"),
            P("sub", "tensor"),
            P(("groups", "stream"), None, ("tensor", "sub")),
            P(("groups", "stream"), None, ("tensor", "sub")),
            P(("groups", "stream"), None, None, None, ("tensor", "sub")),
            P(None, None, ("tensor", "sub")),
            P(("tensor", "sub"), None),
            P(),
            P("groups"),
            P("groups"),
            P("groups"),
        ),
        out_specs=(
            P(("groups", "stream"), "sub"),
            P(("groups", "stream"), None, None, None, ("tensor", "sub")),
        ),
        check_vma=False,
    )
```

```python
import functools

import jax
import jax.numpy as jnp
from jax import lax
from jax.experimental import pallas as pl
from jax.experimental.pallas import tpu as pltpu
from jax.sharding import PartitionSpec as P

D = 3584
QUERY_HEADS = 28
KEY_VALUE_HEADS = 4
HEAD_WIDTH = 128
C = 1024
DHD = 64
SLOTS = 6

LANES = 128
step_size = 0.5
epsilon = 1e-06

VMEM = pl.BlockSpec(memory_space=pltpu.VMEM)
SMEM = pl.BlockSpec(memory_space=pltpu.SMEM)
ANY = pl.BlockSpec(memory_space=pl.ANY)


def grant(*arrays):
    size = sum(
        functools.reduce(lambda x, y: x * y, array.shape, 1) * array.dtype.itemsize
        for array in arrays
    )
    return pltpu.CompilerParams(vmem_limit_bytes=min(60 << 20, size * 5 // 4 + (4 << 20)))


def lm_attend_kernel(unroll, first, lengths, query, cache, fresh, out, wide, result):
    streams, query_width = query.shape
    positions = cache.shape[1]
    key_width = cache.shape[3]
    heads = query_width // HEAD_WIDTH
    groups = key_width // HEAD_WIDTH
    ratio = QUERY_HEADS // KEY_VALUE_HEADS
    stride = -(-streams // 8) * 8
    rows = wide.shape[0] // stride
    wide[...] = jnp.zeros(wide.shape, jnp.float32)
    for head in range(heads):
        lanes = slice(head * HEAD_WIDTH, (head + 1) * HEAD_WIDTH)
        wide[head * stride : head * stride + streams, :] = query[:, lanes].astype(jnp.float32)
    group_of = lax.broadcasted_iota(jnp.int32, (rows, HEAD_WIDTH), 0) // ratio
    extra = 16
    is_new = lax.broadcasted_iota(jnp.int32, (extra, key_width), 0) == 0
    key_at = lax.broadcasted_iota(jnp.int32, (rows, positions + extra), 1)

    def attend(stream):
        queries = wide[pl.ds(stream, rows, stride=stride), :]
        stacked = jnp.concatenate(
            [jnp.where(group_of == group, queries, 0.0) for group in range(groups)], axis=1
        ).astype(jnp.bfloat16)
        pairs = cache[stream].reshape(positions, 2 * key_width)
        pair = fresh[stream].astype(jnp.float32)
        keys = jnp.concatenate(
            [pairs[:, :key_width], jnp.where(is_new, pair[0:1], 0.0).astype(jnp.bfloat16)], axis=0
        )
        values = jnp.concatenate(
            [pairs[:, key_width:], jnp.where(is_new, pair[1:2], 0.0).astype(jnp.bfloat16)], axis=0
        )
        scores = lax.dot_general(
            stacked, keys, (((1,), (1,)), ((), ())), preferred_element_type=jnp.float32
        ) * HEAD_WIDTH ** (-0.5)
        valid = jnp.logical_or(key_at < lengths[first[0] + stream], key_at == positions)
        scores = jnp.where(valid, scores, -1e30)
        top = jnp.max(scores, axis=1, keepdims=True)
        weights = jnp.exp(scores - top)
        total = jnp.sum(weights, axis=1, keepdims=True)
        sums = jnp.dot(weights.astype(jnp.bfloat16), values, preferred_element_type=jnp.float32)
        picked = sums[:, :HEAD_WIDTH]
        for group in range(1, groups):
            lanes = slice(group * HEAD_WIDTH, (group + 1) * HEAD_WIDTH)
            picked = jnp.where(group_of == group, sums[:, lanes], picked)
        result[pl.ds(stream, rows, stride=stride), :] = picked / total

    def step(at, carry):
        for offset in range(unroll):
            attend(at * unroll + offset)
        return carry

    lax.fori_loop(0, streams // unroll, step, 0, unroll=streams == unroll)
    for head in range(heads):
        lanes = slice(head * HEAD_WIDTH, (head + 1) * HEAD_WIDTH)
        out[:, lanes] = result[head * stride : head * stride + streams, :].astype(jnp.bfloat16)


def finish_kernel(span, tokens, per_chunk, chunks, table, live, state, late, *refs):
    out = refs[-1]
    width = state.shape[1]
    is_late = lax.broadcasted_iota(jnp.int32, (tokens, width), 0) == span - 1

    def clear(slot, carry):
        @pl.when(live[slot] == 0)
        def _():
            out[slot] = jnp.zeros((span, width), jnp.bfloat16)
        return carry

    lax.fori_loop(0, out.shape[0], clear, 0)
    terms = len(refs[:-1]) // chunks
    for chunk in range(chunks):
        pieces = refs[chunk * terms : (chunk + 1) * terms]

        def write(at, carry):
            place = chunk * per_chunk + at
            target = table[3, place]

            @pl.when(target >= 0)
            def _():
                slot = table[2, place]
                rows = pl.ds(pl.multiple_of(at * tokens, tokens), tokens)
                mixing = tree_sum([piece[rows, :].astype(jnp.float32) for piece in pieces])
                held = pl.ds(pl.multiple_of(slot * tokens, tokens), tokens)
                span_state = jnp.where(
                    is_late, late[pl.ds(slot, 1), :], state[held, :].astype(jnp.float32)
                )
                updated = step_size * (span_state + mixing)
                out[target] = updated[:span].astype(jnp.bfloat16)
            return carry

        lax.fori_loop(0, per_chunk, write, 0)


def exclusive_rank(hot, reduce_axis):
    return jnp.sum((jnp.cumsum(hot, axis=reduce_axis) - hot) * hot, axis=-1)


def exchange(value, axis, distance):
    return lax.ppermute(value, axis, [(i, i ^ distance) for i in range(lax.axis_size(axis))])


def shift(value, axis, distance):
    size = lax.axis_size(axis)
    return lax.ppermute(value, axis, [(i, (i + distance) % size) for i in range(size)])


def tree_sum(values):
    while len(values) > 1:
        values = [values[i] + values[i + 1] for i in range(0, len(values), 2)]
    return values[0]


def dispatch_kernel(owners, span, tokens, streams, table, noise, pending, cache, *rest):
    states = rest[:owners]
    caches = rest[owners : 2 * owners]
    wide, sems = rest[2 * owners :]
    width = noise.shape[1]

    def copy(slot):
        target = caches[slot // SLOTS].at[slot % SLOTS]
        return pltpu.make_async_copy(cache.at[table[1, slot]], target, sems.at[slot])

    for slot in range(owners * SLOTS):
        copy(slot).start()
    early = (span - 1) * streams
    for part in range(width // LANES):
        lanes = slice(part * LANES, (part + 1) * LANES)
        wide[part, :early] = noise[:early, lanes].astype(jnp.float32) + pending[
            :, lanes
        ].astype(jnp.float32)
        wide[part, early : span * streams] = noise[early:, lanes].astype(jnp.float32)
        wide[part, span * streams :] = jnp.zeros(
            ((tokens - span) * streams, LANES), jnp.float32
        )
        for slot in range(owners * SLOTS):
            rows = wide[part, pl.ds(table[0, slot], tokens, stride=streams), :]
            first = slot % SLOTS * tokens
            states[slot // SLOTS][first : first + tokens, lanes] = rows.astype(jnp.bfloat16)
    for slot in range(owners * SLOTS):
        copy(slot).wait()


def project_kernel(block_rows, piece_count, index, *refs):
    pieces = refs[:piece_count]
    gain, weights, q_out, k_out, v_out = refs[piece_count:]
    width = pieces[0].shape[1]

    def block(step, carry):
        rows = pl.ds(pl.multiple_of(step * block_rows, block_rows), block_rows)
        values = [piece[rows, :].astype(jnp.float32) for piece in pieces]
        squares = functools.reduce(
            jnp.add, [jnp.sum(value * value, axis=1, keepdims=True) for value in values]
        )
        scale = lax.rsqrt(squares / C + epsilon)
        sums = [jnp.zeros((block_rows, width), jnp.float32) for _ in range(3)]
        for at, value in enumerate(values):
            part = index[at]
            normed = (value * scale * gain[part]).astype(jnp.bfloat16)
            features = pl.ds(pl.multiple_of(part * width, width), width)
            for which in range(3):
                sums[which] += jnp.dot(
                    normed, weights[which, features, :], preferred_element_type=jnp.float32
                )
        for out, value in zip((q_out, k_out, v_out), sums):
            out[rows, :] = value.astype(jnp.bfloat16)
        return carry

    lax.fori_loop(0, pieces[0].shape[0] // block_rows, block, 0)


def late_kernel(owners, parts, index, picker, gathered, gain, weights, q_out, k_out, v_out, s_out):
    width = gathered.shape[2]

    def select(part):
        rows = jnp.concatenate(
            [gathered[home * parts + part].astype(jnp.float32) for home in range(owners)], axis=0
        )
        return jnp.dot(
            picker[...], rows.astype(jnp.bfloat16), preferred_element_type=jnp.float32
        )

    values = [select(part) for part in range(parts)]
    squares = functools.reduce(
        jnp.add, [jnp.sum(value * value, axis=1, keepdims=True) for value in values]
    )
    scale = lax.rsqrt(squares / C + epsilon)
    sums = [jnp.zeros((picker.shape[0], width), jnp.float32) for _ in range(3)]
    for part, value in enumerate(values):
        normed = (value * scale * gain[part]).astype(jnp.bfloat16)
        for which in range(3):
            sums[which] += jnp.dot(
                normed,
                weights[which, part * width : (part + 1) * width, :],
                preferred_element_type=jnp.float32,
            )
    for out, value in zip((q_out, k_out, v_out), sums):
        out[...] = value.astype(jnp.bfloat16).astype(jnp.float32)
    s_out[...] = select(index[0])


def attend_kernel(
    shifts, span, tokens, first_place, tensor_count, sub_count,
    index, table, q_rows, k_rows, v_rows, q_late, k_late, v_late, out_weights, *rest,
):
    caches = rest[:shifts]
    keep_out, send_out, keys, values, mixed = rest[shifts:]
    slots, past = caches[0].shape[:2]
    width = q_rows.shape[1]
    heads = width // DHD
    key_rows = keys.shape[1]
    own = key_rows - tokens
    if own > past:
        filler = jnp.zeros((slots, own - past, width), jnp.bfloat16)
        keys[:, past:own, :] = filler
        values[:, past:own, :] = filler
    lane_head = lax.broadcasted_iota(jnp.int32, (tokens, width), 1) // DHD
    late = lax.broadcasted_iota(jnp.int32, (tokens, width), 0) == span - 1
    key_at = lax.broadcasted_iota(jnp.int32, (heads * tokens, key_rows), 1)
    valid = jnp.logical_or(
        key_at < past, jnp.logical_and(key_at >= own, key_at < own + span)
    )

    def with_late(rows_ref, late_ref, slot):
        rows = rows_ref[pl.ds(pl.multiple_of(slot * tokens, tokens), tokens), :]
        return jnp.where(late, late_ref[pl.ds(slot, 1), :], rows.astype(jnp.float32))

    for at in range(shifts * slots):
        buffer = at % slots
        slot = table[2, first_place + at]
        pairs = caches[at // slots][buffer].reshape(past, 2 * width)
        keys[buffer, :past, :] = pairs[:, :width]
        values[buffer, :past, :] = pairs[:, width:]
        keys[buffer, own:, :] = with_late(k_rows, k_late, slot).astype(jnp.bfloat16)
        values[buffer, own:, :] = with_late(v_rows, v_late, slot).astype(jnp.bfloat16)
        queries = with_late(q_rows, q_late, slot) * DHD ** (-0.5)
        stacked = jnp.concatenate(
            [jnp.where(lane_head == head, queries, 0.0) for head in range(heads)], axis=0
        ).astype(jnp.bfloat16)
        scores = lax.dot_general(
            stacked, keys[buffer], (((1,), (1,)), ((), ())), preferred_element_type=jnp.float32
        )
        scores = jnp.where(valid, scores, -1e30)
        top = jnp.max(scores, axis=1, keepdims=True)
        weights = jnp.exp(scores - top)
        total = jnp.sum(weights, axis=1, keepdims=True)
        sums = jnp.dot(
            weights.astype(jnp.bfloat16), values[buffer], preferred_element_type=jnp.float32
        )
        sums = sums * (1.0 / total)
        result = sums[:tokens]
        for head in range(1, heads):
            result = jnp.where(
                lane_head == head, sums[head * tokens : (head + 1) * tokens], result
            )
        mixed[at * tokens : (at + 1) * tokens, :] = result.astype(jnp.bfloat16)
    my_tensor, my_sub = index[0] // sub_count, index[0] % sub_count
    for step in range(tensor_count):
        for out, sub in ((keep_out, my_sub), (send_out, 1 - my_sub)):
            part = jnp.bitwise_xor(my_tensor, step) * sub_count + sub
            lanes = pl.ds(pl.multiple_of(part * width, width), width)
            out[step] = jnp.dot(
                mixed[...], out_weights[:, lanes], preferred_element_type=jnp.float32
            ).astype(out.dtype)


def shards(
    lm_query,
    lm_cache,
    language_new_pair,
    lm_lengths,
    lm_resid,
    lm_wo,
    lm_gain,
    lm_adapt,
    det_noise,
    det_pending,
    det_cache,
    det_qkv,
    det_out,
    det_gain,
    complete,
    owner,
    prev_owner,
):
    owners = lax.axis_size("stream")
    tensor_count = lax.axis_size("tensor")
    sub_count = lax.axis_size("sub")
    parts = tensor_count * sub_count
    home = lax.axis_index("stream")
    my_tensor = lax.axis_index("tensor")
    my_sub = lax.axis_index("sub")
    part_index = my_tensor * sub_count + my_sub
    local_streams = lm_query.shape[0]
    shard_streams, span_len, col_width = det_noise.shape
    past_len = det_cache.shape[2]
    tokens = -(-span_len // 16) * 16
    slot_count = owners * SLOTS
    stream_total = owner.shape[0]

    stream_ids = jnp.arange(stream_total)
    owner_range = jnp.arange(owners)
    done = complete == 1
    owner_hot = jnp.logical_and(owner[:, None] == owner_range[None, :], done[:, None]).astype(
        jnp.int32
    )
    by_home = owner_hot.reshape(owners, shard_streams, owners)
    home_rank = jnp.sum(
        (jnp.cumsum(by_home, axis=1) - by_home).reshape(stream_total, owners) * owner_hot, axis=-1
    )
    prev_hot = (prev_owner[:, None] == owner_range[None, :]).astype(jnp.int32)
    cache_slot = exclusive_rank(prev_hot, 0)
    pair_key = prev_owner * owners + owner
    pair_hot = jnp.logical_and(
        pair_key[:, None] == jnp.arange(owners * owners)[None, :], done[:, None]
    ).astype(jnp.int32)
    pair_rank = exclusive_rank(pair_hot, 0)
    slot_range = jnp.arange(slot_count)
    stream_home = stream_ids // shard_streams
    away = jnp.where(owner >= home, owner - home, owner - home + owners)
    here = jnp.logical_and(done, stream_home == home)
    send_key = jnp.where(here, away * SLOTS + home_rank, -1)
    send_stream = jnp.sum(
        jnp.where(
            slot_range[:, None] == send_key[None, :], (stream_ids % shard_streams)[None, :], 0
        ),
        axis=1,
    )
    moving = jnp.logical_and(done, prev_owner == home)
    cache_key = jnp.where(moving, away * SLOTS + pair_rank, -1)
    send_cache = jnp.sum(
        jnp.where(slot_range[:, None] == cache_key[None, :], cache_slot[None, :], 0), axis=1
    )
    owned = jnp.logical_and(done, owner == home)
    from_home = jnp.where(home >= stream_home, home - stream_home, home - stream_home + owners)
    slot_key = jnp.where(owned, from_home * SLOTS + home_rank, -1)
    out_key = stream_home * SLOTS + home_rank
    from_prev = jnp.where(home >= prev_owner, home - prev_owner, home - prev_owner + owners)
    place_key = jnp.where(owned, from_prev * SLOTS + pair_rank, -1)
    place_hot = slot_range[:, None] == place_key[None, :]
    place_slot = jnp.sum(jnp.where(place_hot, slot_key[None, :], 0), axis=1)
    place_out = jnp.sum(jnp.where(place_hot, out_key[None, :] + 1, 0), axis=1) - 1
    picker = (slot_range[:, None] == slot_key[None, :]).astype(jnp.bfloat16)
    live = jnp.sum(
        jnp.logical_and(slot_range[:, None] == out_key[None, :], owned[None, :]).astype(jnp.int32),
        axis=1,
    )
    table = jnp.stack([send_stream, send_cache, place_slot, place_out]).astype(jnp.int32)

    noise_rows = jnp.transpose(det_noise, (1, 0, 2)).reshape(span_len * shard_streams, col_width)
    pending_rows = jnp.transpose(det_pending, (1, 0, 2)).reshape(-1, col_width)
    shapes = [jax.ShapeDtypeStruct((SLOTS * tokens, col_width), jnp.bfloat16)] * owners
    shapes += [
        jax.ShapeDtypeStruct((SLOTS, past_len, 2, col_width), jnp.bfloat16)
    ] * owners
    packed = pl.pallas_call(
        functools.partial(dispatch_kernel, owners, span_len, tokens, shard_streams),
        out_shape=shapes,
        in_specs=[SMEM, VMEM, VMEM, ANY],
        out_specs=[VMEM] * (2 * owners),
        scratch_shapes=[
            pltpu.VMEM((col_width // LANES, tokens * shard_streams, LANES), jnp.float32),
            pltpu.SemaphoreType.DMA((slot_count,)),
        ],
        compiler_params=grant(noise_rows, pending_rows, det_cache, noise_rows, noise_rows),
        name="dispatch",
    )(table, noise_rows, pending_rows, det_cache.reshape(shard_streams, past_len, 2, col_width))
    arrived = [packed[0]] + [
        shift(packed[step], "stream", step) for step in range(1, owners)
    ]
    caches = [packed[owners]] + [
        shift(packed[owners + step], "stream", step) for step in range(1, owners)
    ]
    state = jnp.concatenate(arrived, axis=0)
    by_tensor = [state] + [exchange(state, "tensor", step) for step in range(1, tensor_count)]
    pieces = []
    piece_index = []
    for step in range(tensor_count):
        for flip in range(sub_count):
            pieces.append(by_tensor[step] if flip == 0 else exchange(by_tensor[step], "sub", flip))
            piece_index.append(
                jnp.bitwise_xor(my_tensor, step) * sub_count + jnp.bitwise_xor(my_sub, flip)
            )
    piece_index = jnp.stack(piece_index).astype(jnp.int32)
    gain_rows = det_gain.astype(jnp.float32).reshape(parts, 1, col_width)
    row_count = slot_count * tokens
    rows_shape = jax.ShapeDtypeStruct((row_count, col_width), jnp.bfloat16)
    q_rows, k_rows, v_rows = pl.pallas_call(
        functools.partial(project_kernel, SLOTS * tokens, parts),
        out_shape=[rows_shape] * 3,
        in_specs=[SMEM] + [VMEM] * (parts + 2),
        out_specs=[VMEM] * 3,
        compiler_params=grant(*pieces, *[rows_shape] * 3, det_qkv),
        name="project",
    )(piece_index, *pieces, gain_rows, det_qkv)

    first = ((home * sub_count + my_sub) * local_streams).astype(jnp.int32).reshape(1)
    lm_query, _ = lax.optimization_barrier((lm_query, packed[0]))
    unroll = 12 if local_streams % 12 == 0 else 1
    stride = -(-local_streams // 8) * 8
    head_rows = -(-(lm_query.shape[1] // HEAD_WIDTH) // 8) * 8
    attention = pl.pallas_call(
        functools.partial(lm_attend_kernel, unroll),
        out_shape=jax.ShapeDtypeStruct(lm_query.shape, jnp.bfloat16),
        in_specs=[SMEM, SMEM, VMEM, VMEM, VMEM],
        out_specs=VMEM,
        scratch_shapes=[pltpu.VMEM((head_rows * stride, HEAD_WIDTH), jnp.float32)] * 2,
        compiler_params=grant(lm_query, lm_cache, lm_query, lm_query, lm_query),
        name="lm_attend",
    )(first, lm_lengths, lm_query, lm_cache, language_new_pair)
    other = exchange(attention, "sub", 1)
    attention_all = jnp.where(
        my_sub == 0,
        jnp.concatenate([attention, other], axis=0),
        jnp.concatenate([other, attention], axis=0),
    )
    partial_out = jnp.dot(attention_all, lm_wo, preferred_element_type=jnp.float32).astype(
        jnp.bfloat16
    )
    terms = [partial_out] + [
        exchange(partial_out, "tensor", step) for step in range(1, tensor_count)
    ]
    product = tree_sum([term.astype(jnp.float32) for term in terms])
    hidden = (lm_resid.astype(jnp.float32) + product).astype(jnp.bfloat16)
    hidden_wide = hidden.astype(jnp.float32)
    square_part = jnp.sum(hidden_wide * hidden_wide, axis=1)
    scaled = (hidden_wide * lm_gain.astype(jnp.float32)[None, :]).astype(jnp.bfloat16)
    cond_part = jnp.dot(scaled, lm_adapt, preferred_element_type=jnp.float32)
    bundle = jnp.concatenate(
        [cond_part, jnp.broadcast_to(square_part[:, None], (shard_streams, LANES))], axis=1
    )
    bundle = bundle + exchange(bundle, "sub", 1)
    tensor_width = lm_adapt.shape[1]
    inverse = lax.rsqrt(bundle[:, tensor_width : tensor_width + 1] / D + epsilon)
    cond_mine = lax.dynamic_slice_in_dim(bundle, my_sub * col_width, col_width, 1)
    cond_new = (cond_mine * inverse).astype(jnp.bfloat16)

    last_state = (
        det_noise[:, span_len - 1].astype(jnp.float32) + cond_new.astype(jnp.float32)
    ).astype(jnp.bfloat16)
    gathered = lax.all_gather(last_state, ("stream", "tensor", "sub"), axis=0)
    late_shape = jax.ShapeDtypeStruct((slot_count, col_width), jnp.float32)
    my_index = part_index.astype(jnp.int32).reshape(1)
    q_late, k_late, v_late, s_late = pl.pallas_call(
        functools.partial(late_kernel, owners, parts),
        out_shape=[late_shape] * 4,
        in_specs=[SMEM] + [VMEM] * 4,
        out_specs=[VMEM] * 4,
        compiler_params=grant(gathered, det_qkv, *[late_shape] * 4),
        name="late",
    )(my_index, picker, gathered, gain_rows, det_qkv)

    shifts = max(1, owners // 4)
    chunk_count = owners // shifts
    chunk_slots = shifts * SLOTS
    chunk_rows = chunk_slots * tokens
    key_rows = -(-past_len // 16) * 16 + tokens
    keep_shape = jax.ShapeDtypeStruct((tensor_count, chunk_rows, col_width), jnp.float32)
    send_shape = jax.ShapeDtypeStruct((tensor_count, chunk_rows, col_width), jnp.bfloat16)
    summed = []
    for chunk in range(chunk_count):
        used = caches[chunk * shifts : (chunk + 1) * shifts]
        if chunk >= 2:
            q_late, _ = lax.optimization_barrier((q_late, summed[chunk - 2][1]))
        keep, send = pl.pallas_call(
            functools.partial(
                attend_kernel, shifts, span_len, tokens, chunk * chunk_slots,
                tensor_count, sub_count,
            ),
            out_shape=[keep_shape, send_shape],
            in_specs=[SMEM] * 2 + [VMEM] * (7 + shifts),
            out_specs=[VMEM] * 2,
            scratch_shapes=[
                pltpu.VMEM((SLOTS, key_rows, col_width), jnp.bfloat16),
                pltpu.VMEM((SLOTS, key_rows, col_width), jnp.bfloat16),
                pltpu.VMEM((chunk_rows, col_width), jnp.bfloat16),
            ],
            compiler_params=grant(*[rows_shape] * 3, *used, keep_shape, send_shape, send_shape),
            name="attend",
        )(my_index, table, q_rows, k_rows, v_rows, q_late, k_late, v_late, det_out, *used)
        both = keep + exchange(send, "sub", 1).astype(jnp.float32)
        summed.append(
            [both[0]]
            + [
                exchange(both[step].astype(jnp.bfloat16), "tensor", step)
                for step in range(1, tensor_count)
            ]
        )
    terms = [term for chunk in summed for term in chunk]
    out_shape = jax.ShapeDtypeStruct((slot_count, span_len, col_width), jnp.bfloat16)
    updated = pl.pallas_call(
        functools.partial(finish_kernel, span_len, tokens, chunk_slots, chunk_count),
        out_shape=out_shape,
        in_specs=[SMEM] * 2 + [VMEM] * (2 + len(terms)),
        out_specs=VMEM,
        compiler_params=grant(state, out_shape, *terms),
        name="finish",
    )(table, live, state, s_late, *terms)
    return (hidden, updated.reshape(1, owners, SLOTS, span_len, col_width))


def solution(mesh):
    return jax.shard_map(
        shards,
        mesh=mesh,
        in_specs=(
            P(("groups", "stream", "sub"), "tensor"),
            P(("groups", "stream", "sub"), None, None, "tensor"),
            P(("groups", "stream", "sub"), None, "tensor"),
            P("groups"),
            P(("groups", "stream"), "sub"),
            P("tensor", "sub"),
            P("sub"),
            P("sub", "tensor"),
            P(("groups", "stream"), None, ("tensor", "sub")),
            P(("groups", "stream"), None, ("tensor", "sub")),
            P(("groups", "stream"), None, None, None, ("tensor", "sub")),
            P(None, None, ("tensor", "sub")),
            P(("tensor", "sub"), None),
            P(),
            P("groups"),
            P("groups"),
            P("groups"),
        ),
        out_specs=(
            P(("groups", "stream"), "sub"),
            P(("groups", "stream"), None, None, None, ("tensor", "sub")),
        ),
        check_vma=False,
    )
```

```python
import functools

import jax
import jax.numpy as jnp
from jax import lax
from jax.experimental import pallas as pl
from jax.experimental.pallas import tpu as pltpu
from jax.sharding import PartitionSpec as P


D = 3584
QUERY_HEADS = 28
KEY_VALUE_HEADS = 4
HEAD_WIDTH = 128
C = 1024
DHD = 64
SLOTS = 6
PADDED_SLOTS = 8

LANES = 128
step_size = 0.5
epsilon = 1e-06

VMEM = pl.BlockSpec(memory_space=pltpu.VMEM)
SMEM = pl.BlockSpec(memory_space=pltpu.SMEM)
HBM = pl.BlockSpec(memory_space=pltpu.HBM)


def grant(*arrays):
    size = sum(
        functools.reduce(lambda x, y: x * y, array.shape, 1) * array.dtype.itemsize
        for array in arrays
    )
    return pltpu.CompilerParams(vmem_limit_bytes=min(60 << 20, size * 5 // 4 + (4 << 20)))


def lm_attend_kernel(unroll, first, lengths, query, cache, fresh, out, wide, result):
    streams, query_width = query.shape
    positions = cache.shape[1]
    key_width = cache.shape[3]
    heads = query_width // HEAD_WIDTH
    groups = key_width // HEAD_WIDTH
    ratio = QUERY_HEADS // KEY_VALUE_HEADS
    stride = -(-streams // 8) * 8
    rows = wide.shape[0] // stride
    wide[...] = jnp.zeros(wide.shape, jnp.float32)
    for head in range(heads):
        lanes = slice(head * HEAD_WIDTH, (head + 1) * HEAD_WIDTH)
        wide[head * stride : head * stride + streams, :] = query[:, lanes].astype(jnp.float32)
    group_of = lax.broadcasted_iota(jnp.int32, (rows, HEAD_WIDTH), 0) // ratio
    extra = 16
    is_new = lax.broadcasted_iota(jnp.int32, (extra, key_width), 0) == 0
    key_at = lax.broadcasted_iota(jnp.int32, (rows, positions + extra), 1)

    def attend(stream):
        queries = wide[pl.ds(stream, rows, stride=stride), :]
        stacked = jnp.concatenate(
            [jnp.where(group_of == group, queries, 0.0) for group in range(groups)], axis=1
        ).astype(jnp.bfloat16)
        pairs = cache[stream].reshape(positions, 2 * key_width)
        pair = fresh[stream].astype(jnp.float32)
        keys = jnp.concatenate(
            [pairs[:, :key_width], jnp.where(is_new, pair[0:1], 0.0).astype(jnp.bfloat16)], axis=0
        )
        values = jnp.concatenate(
            [pairs[:, key_width:], jnp.where(is_new, pair[1:2], 0.0).astype(jnp.bfloat16)], axis=0
        )
        scores = lax.dot_general(
            stacked, keys, (((1,), (1,)), ((), ())), preferred_element_type=jnp.float32
        ) * HEAD_WIDTH ** (-0.5)
        valid = jnp.logical_or(key_at < lengths[first[0] + stream], key_at == positions)
        scores = jnp.where(valid, scores, -1e30)
        top = jnp.max(scores, axis=1, keepdims=True)
        weights = jnp.exp(scores - top)
        total = jnp.sum(weights, axis=1, keepdims=True)
        sums = jnp.dot(weights.astype(jnp.bfloat16), values, preferred_element_type=jnp.float32)
        picked = sums[:, :HEAD_WIDTH]
        for group in range(1, groups):
            lanes = slice(group * HEAD_WIDTH, (group + 1) * HEAD_WIDTH)
            picked = jnp.where(group_of == group, sums[:, lanes], picked)
        result[pl.ds(stream, rows, stride=stride), :] = picked / total

    def step(at, carry):
        for offset in range(unroll):
            attend(at * unroll + offset)
        return carry

    lax.fori_loop(0, streams // unroll, step, 0, unroll=streams == unroll)
    for head in range(heads):
        lanes = slice(head * HEAD_WIDTH, (head + 1) * HEAD_WIDTH)
        out[:, lanes] = result[head * stride : head * stride + streams, :].astype(jnp.bfloat16)


def finish_kernel(span, tokens, per_chunk, chunks, table, live, state, late, *refs):
    out = refs[-1]
    width = state.shape[1]
    is_late = lax.broadcasted_iota(jnp.int32, (tokens, width), 0) == span - 1

    def clear(slot, carry):
        @pl.when(live[slot] == 0)
        def _():
            out[slot] = jnp.zeros((span, width), jnp.bfloat16)

        return carry

    lax.fori_loop(0, out.shape[0], clear, 0)
    terms = len(refs[:-1]) // chunks
    for chunk in range(chunks):
        pieces = refs[chunk * terms : (chunk + 1) * terms]

        def write(at, carry):
            place = chunk * per_chunk + at
            target = table[3, place]

            @pl.when(target >= 0)
            def _():
                slot = table[2, place]
                rows = pl.ds(pl.multiple_of(at * tokens, tokens), tokens)
                mixing = tree_sum([piece[rows, :].astype(jnp.float32) for piece in pieces])
                held = pl.ds(pl.multiple_of(slot * tokens, tokens), tokens)
                span_state = jnp.where(
                    is_late, late[pl.ds(table[4, place], 1), :], state[held, :].astype(jnp.float32)
                )
                updated = step_size * (span_state + mixing)
                out[target] = updated[:span].astype(jnp.bfloat16)

            return carry

        lax.fori_loop(0, per_chunk, write, 0)


def exclusive_rank(hot, reduce_axis):
    return jnp.sum((jnp.cumsum(hot, axis=reduce_axis) - hot) * hot, axis=-1)


def exchange(value, axis, distance):
    return lax.ppermute(value, axis, [(i, i ^ distance) for i in range(lax.axis_size(axis))])


def shift(value, axis, distance):
    size = lax.axis_size(axis)
    return lax.ppermute(value, axis, [(i, (i + distance) % size) for i in range(size)])


def tree_sum(values):
    while len(values) > 1:
        values = [values[i] + values[i + 1] for i in range(0, len(values), 2)]
    return values[0]


def dispatch_kernel(
    owners, span, tokens, streams, table, noise_hbm, pending_hbm, cache, *rest
):
    states = rest[:owners]
    caches = rest[owners : 2 * owners]
    noise, pending, wide, sems, row_sems = rest[2 * owners :]
    width = noise.shape[1]

    def copy(slot):
        target = caches[slot // SLOTS].at[slot % SLOTS]
        return pltpu.make_async_copy(cache.at[table[1, slot]], target, sems.at[slot])

    row_copies = [
        pltpu.make_async_copy(noise_hbm, noise, row_sems.at[0]),
        pltpu.make_async_copy(pending_hbm, pending, row_sems.at[1]),
    ]
    for row_copy in row_copies:
        row_copy.start()
    for slot in range(owners * SLOTS):
        copy(slot).start()
    for row_copy in row_copies:
        row_copy.wait()
    early = (span - 1) * streams
    for part in range(width // LANES):
        lanes = slice(part * LANES, (part + 1) * LANES)
        wide[part, :early] = noise[:early, lanes].astype(jnp.float32) + pending[
            :, lanes
        ].astype(jnp.float32)
        wide[part, early : span * streams] = noise[early:, lanes].astype(jnp.float32)
        wide[part, span * streams :] = jnp.zeros(
            ((tokens - span) * streams, LANES), jnp.float32
        )
        for slot in range(owners * SLOTS):
            rows = wide[part, pl.ds(table[0, slot], tokens, stride=streams), :]
            first = slot % SLOTS * tokens
            states[slot // SLOTS][first : first + tokens, lanes] = rows.astype(jnp.bfloat16)
    for slot in range(owners * SLOTS):
        copy(slot).wait()


def project_kernel(block_rows, piece_count, index, *refs):
    pieces = refs[:piece_count]
    gain, weights, q_out, k_out, v_out = refs[piece_count:]
    width = pieces[0].shape[1]

    def block(step, carry):
        rows = pl.ds(pl.multiple_of(step * block_rows, block_rows), block_rows)
        values = [piece[rows, :].astype(jnp.float32) for piece in pieces]
        squares = functools.reduce(
            jnp.add, [jnp.sum(value * value, axis=1, keepdims=True) for value in values]
        )
        scale = lax.rsqrt(squares / C + epsilon)
        sums = [jnp.zeros((block_rows, width), jnp.float32) for _ in range(3)]
        for at, value in enumerate(values):
            part = index[at]
            normed = (value * scale * gain[part]).astype(jnp.bfloat16)
            features = pl.ds(pl.multiple_of(part * width, width), width)
            for which in range(3):
                sums[which] += jnp.dot(
                    normed, weights[which, features, :], preferred_element_type=jnp.float32
                )
        for out, value in zip((q_out, k_out, v_out), sums):
            out[rows, :] = value.astype(jnp.bfloat16)
        return carry

    lax.fori_loop(0, pieces[0].shape[0] // block_rows, block, 0)


def select_kernel(tensor_count, index, table, *refs):
    halves, outs, rows = refs[:tensor_count], refs[tensor_count:-1], refs[-1]
    width = halves[0].shape[1]
    for step, half in enumerate(halves):
        lanes = pl.ds(pl.multiple_of(jnp.bitwise_xor(index[0], step) * width, width), width)
        rows[:, lanes] = half[...].astype(jnp.float32)
    for away, out in enumerate(outs):
        picked = [rows[pl.ds(table[0, away * SLOTS + slot], 1), :] for slot in range(SLOTS)]
        picked += [picked[0]] * (PADDED_SLOTS - SLOTS)
        out[...] = jnp.concatenate(picked, axis=0).astype(jnp.bfloat16)


def late_kernel(owners, piece_count, span, tokens, index, *refs):
    conds = refs[:owners]
    pieces = refs[owners : owners + piece_count]
    gain, weights, q_out, k_out, v_out, s_out = refs[owners + piece_count :]
    width = pieces[0].shape[1]
    shape = (owners * PADDED_SLOTS, pieces[0].shape[0])
    row = lax.broadcasted_iota(jnp.int32, shape, 0)
    slot = row // PADDED_SLOTS * SLOTS + row % PADDED_SLOTS
    picker = (
        lax.broadcasted_iota(jnp.int32, shape, 1) == slot * tokens + span - 1
    ).astype(jnp.bfloat16)
    values = []
    for at, piece in enumerate(pieces):
        lanes = pl.ds(pl.multiple_of(index[at] * width, width), width)
        noise = jnp.dot(picker, piece[...], preferred_element_type=jnp.float32)
        cond = jnp.concatenate([ref[:, lanes].astype(jnp.float32) for ref in conds], axis=0)
        values.append(noise + cond)
    squares = functools.reduce(
        jnp.add, [jnp.sum(value * value, axis=1, keepdims=True) for value in values]
    )
    scale = lax.rsqrt(squares / C + epsilon)
    sums = [jnp.zeros(values[0].shape, jnp.float32) for _ in range(3)]
    for at, value in enumerate(values):
        part = index[at]
        normed = (value * scale * gain[part]).astype(jnp.bfloat16)
        features = pl.ds(pl.multiple_of(part * width, width), width)
        for which in range(3):
            sums[which] += jnp.dot(
                normed, weights[which, features, :], preferred_element_type=jnp.float32
            )
    for out, value in zip((q_out, k_out, v_out), sums):
        out[...] = value.astype(jnp.bfloat16).astype(jnp.float32)
    s_out[...] = values[0]


def attend_kernel(
    shifts, span, tokens, first_place, tensor_count, sub_count,
    index, table, q_rows, k_rows, v_rows, q_late, k_late, v_late, out_weights, *rest,
):
    caches = rest[:shifts]
    keep_out, send_out, keys, values, mixed = rest[shifts:]
    slots, past = caches[0].shape[:2]
    width = q_rows.shape[1]
    heads = width // DHD
    key_rows = keys.shape[1]
    own = key_rows - tokens
    if own > past:
        filler = jnp.zeros((slots, own - past, width), jnp.bfloat16)
        keys[:, past:own, :] = filler
        values[:, past:own, :] = filler
    lane_head = lax.broadcasted_iota(jnp.int32, (tokens, width), 1) // DHD
    late = lax.broadcasted_iota(jnp.int32, (tokens, width), 0) == span - 1
    key_at = lax.broadcasted_iota(jnp.int32, (heads * tokens, key_rows), 1)
    valid = jnp.logical_or(
        key_at < past, jnp.logical_and(key_at >= own, key_at < own + span)
    )

    def with_late(rows_ref, late_ref, slot, late_row):
        rows = rows_ref[pl.ds(pl.multiple_of(slot * tokens, tokens), tokens), :]
        return jnp.where(late, late_ref[pl.ds(late_row, 1), :], rows.astype(jnp.float32))

    for at in range(shifts * slots):
        buffer = at % slots
        slot = table[2, first_place + at]
        late_row = table[4, first_place + at]
        pairs = caches[at // slots][buffer].reshape(past, 2 * width)
        keys[buffer, :past, :] = pairs[:, :width]
        values[buffer, :past, :] = pairs[:, width:]
        keys[buffer, own:, :] = with_late(k_rows, k_late, slot, late_row).astype(jnp.bfloat16)
        values[buffer, own:, :] = with_late(v_rows, v_late, slot, late_row).astype(jnp.bfloat16)
        queries = with_late(q_rows, q_late, slot, late_row) * DHD ** (-0.5)
        stacked = jnp.concatenate(
            [jnp.where(lane_head == head, queries, 0.0) for head in range(heads)], axis=0
        ).astype(jnp.bfloat16)
        scores = lax.dot_general(
            stacked, keys[buffer], (((1,), (1,)), ((), ())), preferred_element_type=jnp.float32
        )
        scores = jnp.where(valid, scores, -1e30)
        top = jnp.max(scores, axis=1, keepdims=True)
        weights = jnp.exp(scores - top)
        total = jnp.sum(weights, axis=1, keepdims=True)
        sums = jnp.dot(
            weights.astype(jnp.bfloat16), values[buffer], preferred_element_type=jnp.float32
        )
        sums = sums * (1.0 / total)
        result = sums[:tokens]
        for head in range(1, heads):
            result = jnp.where(
                lane_head == head, sums[head * tokens : (head + 1) * tokens], result
            )
        mixed[at * tokens : (at + 1) * tokens, :] = result.astype(jnp.bfloat16)
    my_tensor, my_sub = index[0] // sub_count, index[0] % sub_count
    for step in range(tensor_count):
        for out, sub in ((keep_out, my_sub), (send_out, 1 - my_sub)):
            part = jnp.bitwise_xor(my_tensor, step) * sub_count + sub
            lanes = pl.ds(pl.multiple_of(part * width, width), width)
            out[step] = jnp.dot(
                mixed[...], out_weights[:, lanes], preferred_element_type=jnp.float32
            ).astype(out.dtype)


def shards(
    lm_query,
    lm_cache,
    language_new_pair,
    lm_lengths,
    lm_resid,
    lm_wo,
    lm_gain,
    lm_adapt,
    det_noise,
    det_pending,
    det_cache,
    det_qkv,
    det_out,
    det_gain,
    complete,
    owner,
    prev_owner,
):
    owners = lax.axis_size("stream")
    tensor_count = lax.axis_size("tensor")
    sub_count = lax.axis_size("sub")
    parts = tensor_count * sub_count
    home = lax.axis_index("stream")
    my_tensor = lax.axis_index("tensor")
    my_sub = lax.axis_index("sub")
    part_index = my_tensor * sub_count + my_sub
    local_streams = lm_query.shape[0]
    shard_streams, span_len, col_width = det_noise.shape
    past_len = det_cache.shape[2]
    tokens = -(-span_len // 16) * 16
    slot_count = owners * SLOTS
    stream_total = owner.shape[0]

    complete, owner, prev_owner = lax.optimization_barrier(
        jnp.stack([complete, owner, prev_owner])
    )
    stream_ids = jnp.arange(stream_total)
    owner_range = jnp.arange(owners)
    done = complete == 1
    owner_hot = jnp.logical_and(owner[:, None] == owner_range[None, :], done[:, None]).astype(
        jnp.int32
    )
    by_home = owner_hot.reshape(owners, shard_streams, owners)
    home_rank = jnp.sum(
        (jnp.cumsum(by_home, axis=1) - by_home).reshape(stream_total, owners) * owner_hot, axis=-1
    )
    prev_hot = (prev_owner[:, None] == owner_range[None, :]).astype(jnp.int32)
    cache_slot = exclusive_rank(prev_hot, 0)
    pair_key = prev_owner * owners + owner
    pair_hot = jnp.logical_and(
        pair_key[:, None] == jnp.arange(owners * owners)[None, :], done[:, None]
    ).astype(jnp.int32)
    pair_rank = exclusive_rank(pair_hot, 0)
    slot_range = jnp.arange(slot_count)
    stream_home = stream_ids // shard_streams
    away = jnp.where(owner >= home, owner - home, owner - home + owners)
    here = jnp.logical_and(done, stream_home == home)
    send_key = jnp.where(here, away * SLOTS + home_rank, -1)
    send_stream = jnp.sum(
        jnp.where(
            slot_range[:, None] == send_key[None, :], (stream_ids % shard_streams)[None, :], 0
        ),
        axis=1,
    )
    moving = jnp.logical_and(done, prev_owner == home)
    cache_key = jnp.where(moving, away * SLOTS + pair_rank, -1)
    send_cache = jnp.sum(
        jnp.where(slot_range[:, None] == cache_key[None, :], cache_slot[None, :], 0), axis=1
    )
    owned = jnp.logical_and(done, owner == home)
    from_home = jnp.where(home >= stream_home, home - stream_home, home - stream_home + owners)
    slot_key = jnp.where(owned, from_home * SLOTS + home_rank, -1)
    out_key = stream_home * SLOTS + home_rank
    from_prev = jnp.where(home >= prev_owner, home - prev_owner, home - prev_owner + owners)
    place_key = jnp.where(owned, from_prev * SLOTS + pair_rank, -1)
    place_hot = slot_range[:, None] == place_key[None, :]
    place_slot = jnp.sum(jnp.where(place_hot, slot_key[None, :], 0), axis=1)
    place_out = jnp.sum(jnp.where(place_hot, out_key[None, :] + 1, 0), axis=1) - 1
    place_late = place_slot // SLOTS * PADDED_SLOTS + place_slot % SLOTS
    live = jnp.sum(
        jnp.logical_and(slot_range[:, None] == out_key[None, :], owned[None, :]).astype(jnp.int32),
        axis=1,
    )
    table = jnp.stack([send_stream, send_cache, place_slot, place_out, place_late]).astype(jnp.int32)

    noise_rows = jnp.transpose(det_noise, (1, 0, 2)).reshape(span_len * shard_streams, col_width)
    pending_rows = jnp.transpose(det_pending, (1, 0, 2)).reshape(-1, col_width)
    shapes = [jax.ShapeDtypeStruct((SLOTS * tokens, col_width), jnp.bfloat16)] * owners
    shapes += [
        jax.ShapeDtypeStruct((SLOTS, past_len, 2, col_width), jnp.bfloat16)
    ] * owners
    packed = pl.pallas_call(
        functools.partial(dispatch_kernel, owners, span_len, tokens, shard_streams),
        out_shape=shapes,
        in_specs=[SMEM, HBM, HBM, HBM],
        out_specs=[VMEM] * (2 * owners),
        scratch_shapes=[
            pltpu.VMEM(noise_rows.shape, jnp.bfloat16),
            pltpu.VMEM(pending_rows.shape, jnp.bfloat16),
            pltpu.VMEM((col_width // LANES, tokens * shard_streams, LANES), jnp.float32),
            pltpu.SemaphoreType.DMA((slot_count,)),
            pltpu.SemaphoreType.DMA((2,)),
        ],
        compiler_params=grant(noise_rows, pending_rows, det_cache, noise_rows, noise_rows),
        name="dispatch",
    )(table, noise_rows, pending_rows, det_cache.reshape(shard_streams, past_len, 2, col_width))
    arrived = [packed[0]] + [
        shift(packed[step], "stream", step) for step in range(1, owners)
    ]
    caches = [packed[owners]] + [
        shift(packed[owners + step], "stream", step) for step in range(1, owners)
    ]
    state = jnp.concatenate(arrived, axis=0)
    by_tensor = [state] + [exchange(state, "tensor", step) for step in range(1, tensor_count)]
    pieces = []
    piece_index = []
    for step in range(tensor_count):
        for flip in range(sub_count):
            pieces.append(by_tensor[step] if flip == 0 else exchange(by_tensor[step], "sub", flip))
            piece_index.append(
                jnp.bitwise_xor(my_tensor, step) * sub_count + jnp.bitwise_xor(my_sub, flip)
            )
    piece_index = jnp.stack(piece_index).astype(jnp.int32)
    gain_rows = det_gain.astype(jnp.float32).reshape(parts, 1, col_width)
    row_count = slot_count * tokens
    rows_shape = jax.ShapeDtypeStruct((row_count, col_width), jnp.bfloat16)
    q_rows, k_rows, v_rows = pl.pallas_call(
        functools.partial(project_kernel, SLOTS * tokens, parts),
        out_shape=[rows_shape] * 3,
        in_specs=[SMEM] + [VMEM] * (parts + 2),
        out_specs=[VMEM] * 3,
        compiler_params=grant(*pieces, *[rows_shape] * 3, det_qkv),
        name="project",
    )(piece_index, *pieces, gain_rows, det_qkv)

    first = ((home * sub_count + my_sub) * local_streams).astype(jnp.int32).reshape(1)
    lm_query, _ = lax.optimization_barrier((lm_query, packed[0]))
    unroll = 12 if local_streams % 12 == 0 else 1
    stride = -(-local_streams // 8) * 8
    head_rows = -(-(lm_query.shape[1] // HEAD_WIDTH) // 8) * 8
    attention = pl.pallas_call(
        functools.partial(lm_attend_kernel, unroll),
        out_shape=jax.ShapeDtypeStruct(lm_query.shape, jnp.bfloat16),
        in_specs=[SMEM, SMEM, VMEM, VMEM, VMEM],
        out_specs=VMEM,
        scratch_shapes=[pltpu.VMEM((head_rows * stride, HEAD_WIDTH), jnp.float32)] * 2,
        compiler_params=grant(lm_query, lm_cache, lm_query, lm_query, lm_query),
        name="lm_attend",
    )(first, lm_lengths, lm_query, lm_cache, language_new_pair)
    other = exchange(attention, "sub", 1)
    attention_all = jnp.where(
        my_sub == 0,
        jnp.concatenate([attention, other], axis=0),
        jnp.concatenate([other, attention], axis=0),
    )
    partial_out = jnp.dot(attention_all, lm_wo, preferred_element_type=jnp.float32).astype(
        jnp.bfloat16
    )
    terms = [partial_out] + [
        exchange(partial_out, "tensor", step) for step in range(1, tensor_count)
    ]
    product = tree_sum([term.astype(jnp.float32) for term in terms])
    hidden = (lm_resid.astype(jnp.float32) + product).astype(jnp.bfloat16)
    hidden_wide = hidden.astype(jnp.float32)
    square_part = jnp.sum(hidden_wide * hidden_wide, axis=1)
    scaled = (hidden_wide * lm_gain.astype(jnp.float32)[None, :]).astype(jnp.bfloat16)
    cond_part = jnp.dot(scaled, lm_adapt, preferred_element_type=jnp.float32)
    bundle = jnp.concatenate(
        [cond_part, jnp.broadcast_to(square_part[:, None], (shard_streams, LANES))], axis=1
    )
    bundle = bundle + exchange(bundle, "sub", 1)
    tensor_width = lm_adapt.shape[1]
    inverse = lax.rsqrt(bundle[:, tensor_width : tensor_width + 1] / D + epsilon)
    cond_new = (bundle[:, :tensor_width] * inverse).astype(jnp.bfloat16)
    halves = [cond_new] + [exchange(cond_new, "tensor", step) for step in range(1, tensor_count)]

    cond_shape = jax.ShapeDtypeStruct((PADDED_SLOTS, C), jnp.bfloat16)
    chosen = pl.pallas_call(
        functools.partial(select_kernel, tensor_count),
        out_shape=[cond_shape] * owners,
        in_specs=[SMEM] * 2 + [VMEM] * tensor_count,
        out_specs=[VMEM] * owners,
        scratch_shapes=[pltpu.VMEM((shard_streams, C), jnp.float32)],
        compiler_params=grant(cond_shape),
        name="select",
    )(my_tensor.astype(jnp.int32).reshape(1), table, *halves)
    conds = [chosen[0]] + [shift(chosen[step], "stream", step) for step in range(1, owners)]
    late_shape = jax.ShapeDtypeStruct((owners * PADDED_SLOTS, col_width), jnp.float32)
    my_index = part_index.astype(jnp.int32).reshape(1)
    q_late, k_late, v_late, s_late = pl.pallas_call(
        functools.partial(late_kernel, owners, parts, span_len, tokens),
        out_shape=[late_shape] * 4,
        in_specs=[SMEM] + [VMEM] * (owners + parts + 2),
        out_specs=[VMEM] * 4,
        compiler_params=grant(*pieces, det_qkv, *[late_shape] * 4),
        name="late",
    )(piece_index, *conds, *pieces, gain_rows, det_qkv)

    shifts = max(1, owners // 4)
    chunk_count = owners // shifts
    chunk_slots = shifts * SLOTS
    chunk_rows = chunk_slots * tokens
    key_rows = -(-past_len // 16) * 16 + tokens
    keep_shape = jax.ShapeDtypeStruct((tensor_count, chunk_rows, col_width), jnp.float32)
    send_shape = jax.ShapeDtypeStruct((tensor_count, chunk_rows, col_width), jnp.bfloat16)
    summed = []
    for chunk in range(chunk_count):
        used = caches[chunk * shifts : (chunk + 1) * shifts]
        if chunk >= 2:
            q_late, _ = lax.optimization_barrier((q_late, summed[chunk - 2][1]))
        keep, send = pl.pallas_call(
            functools.partial(
                attend_kernel, shifts, span_len, tokens, chunk * chunk_slots,
                tensor_count, sub_count,
            ),
            out_shape=[keep_shape, send_shape],
            in_specs=[SMEM] * 2 + [VMEM] * (7 + shifts),
            out_specs=[VMEM] * 2,
            scratch_shapes=[
                pltpu.VMEM((SLOTS, key_rows, col_width), jnp.bfloat16),
                pltpu.VMEM((SLOTS, key_rows, col_width), jnp.bfloat16),
                pltpu.VMEM((chunk_rows, col_width), jnp.bfloat16),
            ],
            compiler_params=grant(*[rows_shape] * 3, *used, keep_shape, send_shape, send_shape),
            name="attend",
        )(my_index, table, q_rows, k_rows, v_rows, q_late, k_late, v_late, det_out, *used)
        both = keep + exchange(send, "sub", 1).astype(jnp.float32)
        summed.append(
            [both[0]]
            + [
                exchange(both[step].astype(jnp.bfloat16), "tensor", step)
                for step in range(1, tensor_count)
            ]
        )
    terms = [term for chunk in summed for term in chunk]
    out_shape = jax.ShapeDtypeStruct((slot_count, span_len, col_width), jnp.bfloat16)
    updated = pl.pallas_call(
        functools.partial(finish_kernel, span_len, tokens, chunk_slots, chunk_count),
        out_shape=out_shape,
        in_specs=[SMEM] * 2 + [VMEM] * (2 + len(terms)),
        out_specs=VMEM,
        compiler_params=grant(state, out_shape, *terms),
        name="finish",
    )(table, live, state, s_late, *terms)
    return (hidden, updated.reshape(1, owners, SLOTS, span_len, col_width))


def solution(mesh):
    return jax.shard_map(
        shards,
        mesh=mesh,
        in_specs=(
            P(("groups", "stream", "sub"), "tensor"),
            P(("groups", "stream", "sub"), None, None, "tensor"),
            P(("groups", "stream", "sub"), None, "tensor"),
            P("groups"),
            P(("groups", "stream"), "sub"),
            P("tensor", "sub"),
            P("sub"),
            P("sub", "tensor"),
            P(("groups", "stream"), None, ("tensor", "sub")),
            P(("groups", "stream"), None, ("tensor", "sub")),
            P(("groups", "stream"), None, None, None, ("tensor", "sub")),
            P(None, None, ("tensor", "sub")),
            P(("tensor", "sub"), None),
            P(),
            P("groups"),
            P("groups"),
            P("groups"),
        ),
        out_specs=(
            P(("groups", "stream"), "sub"),
            P(("groups", "stream"), None, None, None, ("tensor", "sub")),
        ),
        check_vma=False,
    )
```
